32 devices in a mesh: grid: 16 (over z, y, core), hel: 2 (over x).
Axes of the slice: x: 2, y: 2, z: 4, core: 2. Of those that a mesh axis runs over, the one named last changes fastest.
Arguments:
- packet_prev: float32 [2, 1024, 5120], P('hel', 'grid'), may hold values from -6 to 6
- packet_now: float32 [2, 1024, 5120], P('hel', 'grid'), may hold values from -6 to 6
- angular_table: float32 [2, 1024, 1536], P('hel', None, 'grid'), may hold values from -0.15625 to 0.15625
- potential: float32 [1536, 5120], P(None, 'grid'), may hold values from 0 to 2
- rotation: float32 [2, 1024], P('hel', 'grid'), may hold values from 0.05 to 1
- radial_weight: float32 [64], replicated, may hold values from 0.5 to 2
- coupling: float32 [2, 1024], P('hel', 'grid'), may hold values from -0.6 to 0.6
- centrifugal: float32 [80], replicated, may hold values from 0.5 to 1.5
Outputs:
- packet_mid: float32 [2, 1024, 5120], P('hel', 'grid')
- packet_last: float32 [2, 1024, 5120], P('hel', 'grid')
The draws below stay inside these ranges and needn't reach their ends.
All inputs are finite; a program needn't handle non-finite values.
Results may differ from the reference program's by a relative error of at most 0.0001.
Values sent between devices are 32-bit elements; how exact they have to be, the bound alone decides.
No kernel may reach another device: no remote copies, remote signals or barrier semaphores. Data moves between devices by JAX's collectives and lax.ppermute only.
A program may use at most 128 MiB of HBM per device.

```python
import math
import jax
import jax.numpy as jnp
from jax import lax

J = 1024
Q = 1536
RB = 80
RS = 64
STEPS = 2
K = 2
NR = 5120


def levels(key, shape, cuts, least, largest):
    def one(axis_at, parts):
        heights = jax.random.uniform(jax.random.fold_in(jax.random.fold_in(key, 6), axis_at), (parts,), jnp.float32, least / len(cuts), largest / len(cuts))
        return jnp.repeat(jnp.exp(heights), shape[axis_at] // parts).reshape((-1,) + (1,) * (len(shape) - axis_at - 1))

    factor_of = one(*cuts[0])
    for cut in cuts[1:]:
        factor_of = factor_of * one(*cut)
    return factor_of


def gaussian(own_key, shape, spread, most, pieces=(), kind=jnp.bfloat16):
    loudness = levels(own_key, shape, pieces, -0.22, 0.18) if pieces else 1.0
    drawn = jax.random.normal(own_key, shape, jnp.float32) * spread * loudness
    return jnp.minimum(jnp.maximum(drawn, -most), most).astype(kind)


def setup_inputs(seed: int = 0) -> dict:
    arg_keys = jax.random.split(jax.random.key(seed), 9)
    packet_prev = gaussian(arg_keys[0], (K, J, NR), 1.0, 6.0, ((0, 2), (1, 16)), jnp.float32)
    packet_now = gaussian(arg_keys[1], (K, J, NR), 1.0, 6.0, ((0, 2), (1, 16)), jnp.float32)
    angular_table = gaussian(arg_keys[2], (K, J, Q), Q ** -0.5, 0.15625, ((0, 2), (2, 16)), jnp.float32)
    potential = jnp.clip(2.0 * jax.random.uniform(arg_keys[3], (Q, NR), jnp.float32) ** levels(arg_keys[3], (Q, NR), ((1, 16),), -0.2, 0.2), 0.0, 2.0)
    rotation = jnp.clip(jnp.exp(math.log(1.0) - 2.9957323 * jax.random.uniform(arg_keys[4], (K, J), jnp.float32) ** levels(arg_keys[4], (K, J), ((0, 2), (1, 16)), -0.2, 0.2)), 0.05, 1.0)
    radial_weight = jnp.clip(jax.random.uniform(arg_keys[5], (RS,), jnp.float32, 0.5, 2.0), 0.5, 2.0)
    coupling = jnp.clip(jax.random.uniform(arg_keys[6], (K, J), jnp.float32, -0.6, 0.6) * levels(arg_keys[6], (K, J), ((0, 2), (1, 16)), -0.4, 0.0), -0.6, 0.6)
    centrifugal = jnp.clip(jax.random.uniform(arg_keys[7], (RB,), jnp.float32, 0.5, 1.5), 0.5, 1.5)
    return dict(packet_prev=packet_prev, packet_now=packet_now, angular_table=angular_table, potential=potential, rotation=rotation, radial_weight=radial_weight, coupling=coupling, centrifugal=centrifugal)


big_scale = 0.05
small_scale = 0.08
centre = 1.0
half_width = 1.5


def kinetic(count, coef):
    index = jnp.arange(count)
    offset = index[:, None] - index[None, :]
    parity = (1 - 2 * (jnp.abs(offset) % 2)).astype(jnp.float32)
    square = jnp.maximum(offset * offset, 1).astype(jnp.float32)
    return coef * jnp.where(offset == 0, jnp.float32(jnp.pi ** 2 / 3.0), 2.0 * parity / square)


def hamiltonian(packet, angular_table, potential, rotation, radial_weight, coupling, centrifugal, kin_big, kin_small):
    high = lax.Precision.HIGHEST
    grid4 = packet.reshape(K, J, RB, RS)
    radial = jnp.einsum('ab,kjbs->kjas', kin_big, grid4, precision=high)
    radial = radial + jnp.einsum('st,kjat->kjas', kin_small, grid4, precision=high)
    radial = radial.reshape(K, J, NR)
    rotational = rotation[:, :, None] * jnp.tile(radial_weight, RB)[None, None, :] * packet
    points = jnp.einsum('kjq,kjn->kqn', angular_table, packet, precision=high)
    back = jnp.einsum('kjq,kqn->kjn', angular_table, points * potential[None], precision=high)
    link = coupling[:, :, None] * jnp.repeat(centrifugal, RS)[None, None, :]
    zeros = jnp.zeros_like(packet[:1])
    below = jnp.concatenate([zeros, packet[:-1]], axis=0)
    scaled = link * packet
    above = jnp.concatenate([scaled[1:], zeros], axis=0)
    coriolis = link * below + above
    return (radial + rotational + back + coriolis - centre * packet) / half_width


def reference(packet_prev, packet_now, angular_table, potential, rotation, radial_weight, coupling, centrifugal):
    kin_big = kinetic(RB, big_scale)
    kin_small = kinetic(RS, small_scale)
    older, newer = packet_prev, packet_now
    for step in range(STEPS):
        applied = hamiltonian(newer, angular_table, potential, rotation, radial_weight, coupling, centrifugal, kin_big, kin_small)
        older, newer = newer, 2.0 * applied - older
    return older, newer
```

```python
import jax
import jax.numpy as jnp
from jax import lax
from jax.sharding import PartitionSpec as P

STEPS = 2

big_scale = 0.05
small_scale = 0.08
centre = 1.0
half_width = 1.5
LANES = 128


def from_behind(shard, axis, by):
    size = lax.axis_size(axis)
    pairs = [(i, i + by) for i in range(size) if 0 <= i + by < size]
    return lax.ppermute(shard, axis, pairs)


def kinetic(count, coef):
    index = jnp.arange(count)
    offset = index[:, None] - index[None, :]
    parity = (1 - 2 * (jnp.abs(offset) % 2)).astype(jnp.float32)
    square = jnp.maximum(offset * offset, 1).astype(jnp.float32)
    return coef * jnp.where(offset == 0, jnp.float32(jnp.pi**2 / 3.0), 2.0 * parity / square)


def pack(blocks):
    G, r, n = blocks.shape
    full = n // LANES * LANES
    rest = n - full
    if not rest or LANES % rest or r % (LANES // rest):
        return blocks
    k = LANES // rest
    parts = [blocks[:, :, i : i + LANES] for i in range(0, full, LANES)]
    tail = blocks[:, :, full:].reshape(G, k, r // k, rest)
    parts.append(jnp.concatenate([tail[:, i] for i in range(k)], axis=2))
    return jnp.concatenate(parts, axis=1)


def unpack(packed, r, n):
    if packed.shape[1:] == (r, n):
        return packed
    full = n // LANES * LANES
    rest = n - full
    k = LANES // rest
    parts = [packed[:, i * r : (i + 1) * r] for i in range(full // LANES)]
    tail = packed[:, full // LANES * r :]
    parts.append(jnp.concatenate([tail[:, :, i * rest : (i + 1) * rest] for i in range(k)], axis=1))
    return jnp.concatenate(parts, axis=2)


def exchange(blocks):
    return lax.all_to_all(blocks, "grid", split_axis=0, concat_axis=0, tiled=True)


def shards(
    packet_prev,
    packet_now,
    angular_table,
    potential,
    rotation,
    radial_weight,
    coupling,
    centrifugal,
):
    high = lax.Precision.HIGH
    G = lax.axis_size("grid")
    K = lax.axis_size("hel")
    RB = centrifugal.shape[0]
    RS = radial_weight.shape[0]
    jl, nr = packet_now.shape[1:]
    nl = nr // G
    c = 2.0 / half_width
    kin_big = kinetic(RB, big_scale)
    kin_small = kinetic(RS, small_scale)

    prev, now = packet_prev[0], packet_now[0]
    table = lax.all_gather(angular_table, "grid", axis=2, tiled=True)[0]
    coup_above = from_behind(coupling, "hel", -1)[0]
    coup = coupling[0]
    diag = rotation[0][:, None] * jnp.tile(radial_weight, RB)[None, :] - centre
    cent = jnp.repeat(centrifugal, RS)[None, :]

    def spread(x):
        got = exchange(pack(x.reshape(jl, G, nl).transpose(1, 0, 2)))
        return unpack(got, jl, nl).reshape(G * jl, nl)

    def collect(x):
        got = exchange(pack(x.reshape(G, jl, nl)))
        return unpack(got, jl, nl).transpose(1, 0, 2).reshape(jl, nr)

    def neighbours(x):
        if K == 2:
            k = lax.axis_index("hel")
            got = lax.ppermute(x, "hel", [(0, 1), (1, 0)])
            return (jnp.where(k == 0, coup_above, coup)[:, None] * cent) * got
        below = from_behind(x, "hel", 1)
        above = from_behind(x, "hel", -1)
        return (coup[:, None] * cent) * below + (coup_above[:, None] * cent) * above

    def radial(x):
        grid3 = x.reshape(jl, RB, RS)
        out = jnp.einsum("ab,jbs->jas", kin_big, grid3, precision=high)
        out = out + jnp.einsum("st,jat->jas", kin_small, grid3, precision=high)
        return out.reshape(jl, nr)

    def local(x):
        return c * (radial(x) + diag * x + neighbours(x))

    def angular(x):
        points = lax.dot_general(table, x, (((0,), (0,)), ((), ())), precision=high)
        return jnp.dot(table, points * potential, precision=high)

    older, newer = prev, now
    newer_points = spread(newer)
    older_points = None
    for step in range(STEPS - 1):
        w = local(newer) - older
        w_points = spread(w)
        newer_points, older_points = w_points + c * angular(newer_points), newer_points
        older, newer = newer, collect(newer_points)
    back = collect(c * angular(newer_points))
    older, newer = newer, local(newer) - older + back
    return older[None], newer[None]


def solution(mesh):
    return jax.shard_map(
        shards,
        mesh=mesh,
        in_specs=(
            P("hel", "grid", None),
            P("hel", "grid", None),
            P("hel", None, "grid"),
            P(None, "grid"),
            P("hel", "grid"),
            P(),
            P("hel", "grid"),
            P(),
        ),
        out_specs=(P("hel", "grid", None), P("hel", "grid", None)),
        check_vma=False,
    )
```

```python
import jax
import jax.numpy as jnp
from jax import lax
from jax.experimental import pallas as pl
from jax.experimental.pallas import tpu as pltpu
from jax.sharding import PartitionSpec as P

STEPS = 2

big_scale = 0.05
small_scale = 0.08
centre = 1.0
half_width = 1.5
LANES = 128


def from_behind(shard, axis, by):
    size = lax.axis_size(axis)
    pairs = [(i, i + by) for i in range(size) if 0 <= i + by < size]
    return lax.ppermute(shard, axis, pairs)


def kinetic(count, coef):
    index = jnp.arange(count)
    offset = index[:, None] - index[None, :]
    parity = (1 - 2 * (jnp.abs(offset) % 2)).astype(jnp.float32)
    square = jnp.maximum(offset * offset, 1).astype(jnp.float32)
    return coef * jnp.where(offset == 0, jnp.float32(jnp.pi**2 / 3.0), 2.0 * parity / square)


def swap_halves(x):
    return pltpu.roll(x, LANES // 2, axis=1)


def low_half(shape):
    return lax.broadcasted_iota(jnp.int32, shape, 1) < LANES // 2


class Packing:
    def __init__(self, G, rows, cols):
        self.G, self.rows, self.cols = G, rows, cols
        self.m = cols // LANES
        self.half = rows // 2
        self.height = self.m * rows + self.half
        self.steps = 2 if (G // 2) % 2 == 0 else 1
        self.pairs = G // 2 // self.steps
        self.width = self.pairs * 2 * cols

    @staticmethod
    def fits(G, rows, cols):
        return G % 2 == 0 and cols % LANES == LANES // 2 and rows % 16 == 0

    def tiles(self, i):
        base = i * 2 * self.cols
        return [base + t * LANES for t in range(2 * self.m + 1)]

    def put(self, o_ref, i, x):
        m, rows, half = self.m, self.rows, self.half
        at = self.tiles(i)
        for t in range(m):
            o_ref[2 * i, t * rows : (t + 1) * rows] = x(at[t])
            o_ref[2 * i + 1, t * rows : (t + 1) * rows] = x(at[m + 1 + t])
        mid = x(at[m])
        top, low = mid[:half], mid[half:]
        lo = low_half(top.shape)
        o_ref[2 * i, m * rows :] = jnp.where(lo, top, swap_halves(low))
        o_ref[2 * i + 1, m * rows :] = jnp.where(lo, swap_halves(top), low)

    def get(self, p_ref, i):
        m, rows = self.m, self.rows
        at = self.tiles(i)
        out = []
        for t in range(m):
            out.append((at[t], p_ref[2 * i, t * rows : (t + 1) * rows]))
            out.append((at[m + 1 + t], p_ref[2 * i + 1, t * rows : (t + 1) * rows]))
        even, odd = p_ref[2 * i, m * rows :], p_ref[2 * i + 1, m * rows :]
        lo = low_half(even.shape)
        top = jnp.where(lo, even, swap_halves(odd))
        low = jnp.where(lo, swap_halves(even), odd)
        out.append((at[m], jnp.concatenate([top, low], axis=0)))
        return out

    def cut(self):
        wide = pl.BlockSpec((self.rows, self.width), lambda s: (0, s))
        packed = pl.BlockSpec((2 * self.pairs, self.height, LANES), lambda s: (s, 0, 0))
        column = pl.BlockSpec((self.rows, 1), lambda s: (0, 0))
        row = pl.BlockSpec((1, self.width), lambda s: (0, s))
        return wide, packed, column, row

    @property
    def packed_shape(self):
        return jax.ShapeDtypeStruct((self.G, self.height, LANES), jnp.float32)

    @property
    def wide_shape(self):
        return jax.ShapeDtypeStruct((self.rows, self.G * self.cols), jnp.float32)

    def pack(self, x):
        def body(x_ref, o_ref):
            for i in range(self.pairs):
                self.put(o_ref, i, lambda at: x_ref[:, at : at + LANES])

        wide, packed, _, _ = self.cut()
        return pl.pallas_call(
            body, grid=(self.steps,), in_specs=[wide], out_specs=packed, out_shape=self.packed_shape, name="pack"
        )(x)

    def pack_linked(self, base, got, factor, cent):
        flat = got.ndim == 2

        def body(b_ref, g_ref, f_ref, c_ref, o_ref):
            f = f_ref[...]
            for i in range(self.pairs):
                tiles = {} if flat else dict(self.get(g_ref, i))
                self.put(
                    o_ref,
                    i,
                    lambda at: b_ref[:, at : at + LANES]
                    + (f * c_ref[:, at : at + LANES]) * (g_ref[:, at : at + LANES] if flat else tiles[at]),
                )

        wide, packed, column, row = self.cut()
        return pl.pallas_call(
            body,
            grid=(self.steps,),
            in_specs=[wide, wide if flat else packed, column, row],
            out_specs=packed,
            out_shape=self.packed_shape,
            name="pack_linked",
        )(base, got, factor, cent)

    def unpack(self, p):
        def body(p_ref, o_ref):
            for i in range(self.pairs):
                for at, tile in self.get(p_ref, i):
                    o_ref[:, at : at + LANES] = tile

        wide, packed, _, _ = self.cut()
        return pl.pallas_call(
            body, grid=(self.steps,), in_specs=[packed], out_specs=wide, out_shape=self.wide_shape, name="unpack"
        )(p)

    def unpack_linked(self, p, base, got, factor, cent):
        flat = got.ndim == 2

        def body(p_ref, b_ref, g_ref, f_ref, c_ref, o_ref):
            f = f_ref[...]
            for i in range(self.pairs):
                tiles = {} if flat else dict(self.get(g_ref, i))
                for at, tile in self.get(p_ref, i):
                    s = slice(at, at + LANES)
                    o_ref[:, s] = b_ref[:, s] + (f * c_ref[:, s]) * (g_ref[:, s] if flat else tiles[at]) + tile

        wide, packed, column, row = self.cut()
        return pl.pallas_call(
            body,
            grid=(self.steps,),
            in_specs=[packed, wide, wide if flat else packed, column, row],
            out_specs=wide,
            out_shape=self.wide_shape,
            name="unpack_linked",
        )(p, base, got, factor, cent)


def split(x):
    high = x.astype(jnp.bfloat16)
    return high, (x - high.astype(jnp.float32)).astype(jnp.bfloat16)


def three(a, b, dims):
    dot = lambda x, y: lax.dot_general(x, y, (dims, ((), ())), preferred_element_type=jnp.float32)
    return dot(a[0], b[0]) + (dot(a[0], b[1]) + dot(a[1], b[0]))


class Angular:
    def __init__(self, form, ql, chunk):
        self.form, self.ql, self.chunk = form, ql, chunk
        self.J = form.G * form.rows
        self.half_q = ql * form.G // 2

    def blocks(self, p_ref, i):
        f = self.form
        m, rows = f.m, f.rows
        for t in range(m):
            yield jnp.concatenate([p_ref[g, t * rows : (t + 1) * rows] for g in (2 * i, 2 * i + 1)], axis=0)
        tails = [p_ref[g, m * rows :] for g in (2 * i, 2 * i + 1)]
        yield jnp.concatenate([tails[0], swap_halves(tails[0]), tails[1], swap_halves(tails[1])], axis=0)

    def call(self, where, packed, tables, pot, acc=None, plus=None, scale=None):
        f = self.form
        m, rows, half, cols, ql, chunk = f.m, f.rows, f.half, f.cols, self.ql, self.chunk
        finish = scale is not None
        wide = 2 * rows

        def body(where_ref, p_ref, t1_ref, t2_ref, pot_ref, *refs):
            refs = list(refs)
            acc_ref = refs.pop(0) if acc is not None else None
            plus_ref = refs.pop(0) if plus is not None else None
            o_ref, xh, xl, th, tl = refs
            for i in range(f.G // 2):
                lanes = slice(i * wide, (i + 1) * wide)
                for t, tile in enumerate(self.blocks(p_ref, i)):
                    turned = tile.T
                    if t == m:
                        turned = turned[: LANES // 2]
                    r = slice(t * LANES, t * LANES + turned.shape[0])
                    xh[r, lanes], xl[r, lanes] = split(turned)
            base = where_ref[1]
            for ref, flips in ((t1_ref, (0, 4, 2, 6)), (t2_ref, (1, 5, 3, 7))):
                for b, flip in enumerate(flips):
                    at = pl.ds(pl.multiple_of((base ^ flip) * ql, 16), ql)
                    th[at, :], tl[at, :] = split(ref[b * ql : (b + 1) * ql, :])
            x = (xh[...], xl[...])
            total = None if acc_ref is None else acc_ref[...]
            for q in range(0, self.half_q, chunk):
                t = (th[q : q + chunk], tl[q : q + chunk])
                points = three(x, t, ((1,), (1,))) * pot_ref[:, q : q + chunk]
                back = three(split(points), t, ((1,), (0,)))
                total = back if total is None else total + back
            if not finish:
                o_ref[...] = total
                return
            for i in range(f.G // 2):
                lanes = slice(i * wide, (i + 1) * wide)

                def store(g, at, value):
                    value = scale * value
                    if plus_ref is not None:
                        value = plus_ref[g, at : at + value.shape[0]] + value
                    o_ref[g, at : at + value.shape[0]] = value

                for t in range(m):
                    tile = total[t * LANES : (t + 1) * LANES, lanes].T
                    store(2 * i, t * rows, tile[:rows])
                    store(2 * i + 1, t * rows, tile[rows:])
                tail = total[m * LANES :, lanes]
                tail = jnp.concatenate([tail, tail], axis=0).T
                lo = low_half((half, LANES))
                for g in (0, 1):
                    at = g * rows
                    store(2 * i + g, m * rows, jnp.where(lo, tail[at : at + half], tail[at + half : at + rows]))

        J = self.J
        whole = lambda shape: pl.BlockSpec(shape, lambda s, w: (0,) * len(shape))
        packed_spec = whole(f.packed_shape.shape)
        in_specs = [packed_spec, whole(tables[0].shape), whole(tables[1].shape)]
        in_specs.append(pl.BlockSpec((cols, self.half_q), lambda s, w: (0, w[0])))
        args = [where, packed, *tables, pot]
        if acc is not None:
            in_specs.append(whole((cols, J)))
            args.append(acc)
        if plus is not None:
            in_specs.append(packed_spec)
            args.append(plus)
        out_shape = f.packed_shape if finish else jax.ShapeDtypeStruct((cols, J), jnp.float32)
        flops = 12 * J * cols * self.half_q
        return pl.pallas_call(
            body,
            out_shape=out_shape,
            grid_spec=pltpu.PrefetchScalarGridSpec(
                num_scalar_prefetch=1,
                grid=(1,),
                in_specs=in_specs,
                out_specs=packed_spec if finish else whole((cols, J)),
                scratch_shapes=[
                    pltpu.VMEM((cols, J), jnp.bfloat16),
                    pltpu.VMEM((cols, J), jnp.bfloat16),
                    pltpu.VMEM((self.half_q, J), jnp.bfloat16),
                    pltpu.VMEM((self.half_q, J), jnp.bfloat16),
                ],
            ),
            cost_estimate=pl.CostEstimate(flops=flops, transcendentals=0, bytes_accessed=8 * J * self.half_q),
            name="angular",
        )(*args)


class Plain:
    def __init__(self, G, rows, cols):
        self.G, self.rows, self.cols = G, rows, cols

    def pack(self, x):
        return x.reshape(self.rows, self.G, self.cols).transpose(1, 0, 2)

    def pack_linked(self, base, got, factor, cent):
        got = got if got.ndim == 2 else self.unpack(got)
        return self.pack(base + (factor * cent) * got)

    def unpack(self, p):
        return p.transpose(1, 0, 2).reshape(self.rows, self.G * self.cols)

    def unpack_linked(self, p, base, got, factor, cent):
        got = got if got.ndim == 2 else self.unpack(got)
        return base + (factor * cent) * got + self.unpack(p)

    def pack_rows(self, x, scale, plus=None):
        x = scale * x.reshape(self.G, self.rows, self.cols)
        return x if plus is None else plus + x

    def unpack_rows(self, p):
        return p.reshape(self.G * self.rows, self.cols)


def exchange(blocks):
    return lax.all_to_all(blocks, "grid", split_axis=0, concat_axis=0, tiled=True)


def gather_table(own):
    G = lax.axis_size("grid")
    me = lax.axis_index("grid")
    z, r = me // 4, me % 4

    def line(x, pairs):
        return lax.ppermute(x, "grid", [(a * 4 + i, b * 4 + i) for a, b in pairs for i in range(4)])

    def flip(x, bit):
        return lax.ppermute(x, "grid", [(i, i ^ bit) for i in range(G)])

    middle = [(1, 2), (2, 1)]
    outward = [(1, 0), (2, 3)]
    near = line(own, [(0, 1), (1, 0), (2, 3), (3, 2)])
    far_in = line(own, middle)
    own_y = flip(own, 2)
    far2_in = line(near, middle)
    near_y = flip(near, 2)
    far_out = line(far_in, outward)
    far2_out = line(far2_in, outward)
    inner = (z == 1) | (z == 2)
    far = jnp.where(inner, far_in, far_out)
    far_y = flip(far, 2)
    far2 = jnp.where(inner, far2_in, far2_out)
    far2_y = flip(far2, 2)
    first = jnp.concatenate([own, near, own_y, near_y])
    first_c = flip(first, 1)
    second = jnp.concatenate([far, far2, far_y, far2_y])
    second_c = flip(second, 1)
    first_at = jnp.stack([z // 2, me % 8]).astype(jnp.int32)
    second_at = jnp.stack([1 - z // 2, jnp.where(z < 2, 0, 4) + r]).astype(jnp.int32)
    return (first_at, (first, first_c)), (second_at, (second, second_c))


def shards(
    packet_prev,
    packet_now,
    angular_table,
    potential,
    rotation,
    radial_weight,
    coupling,
    centrifugal,
):
    high = lax.Precision.HIGH
    G = lax.axis_size("grid")
    K = lax.axis_size("hel")
    RB = centrifugal.shape[0]
    RS = radial_weight.shape[0]
    jl, nr = packet_now.shape[1:]
    nl = nr // G
    c = 2.0 / half_width
    kin_big = kinetic(RB, big_scale)
    kin_small = kinetic(RS, small_scale)

    prev, now = packet_prev[0], packet_now[0]
    coup_above = from_behind(coupling, "hel", -1)[0]
    coup = coupling[0]
    k = lax.axis_index("hel")
    diag = rotation[0][:, None] * jnp.tile(radial_weight, RB)[None, :] - centre
    cent = jnp.repeat(centrifugal, RS)[None, :]
    ql = angular_table.shape[2]
    packs = G == 16 and Packing.fits(G, jl, nl) and ql % 16 == 0 and (8 * ql) % 256 == 0
    form = (Packing if packs else Plain)(G, jl, nl)
    if packs:
        odd = lax.axis_index("grid") % 2 == 1
        turned = jnp.concatenate([potential[:, LANES // 2 :], potential[:, : LANES // 2]], axis=1)
        pot = jnp.where(odd, turned, potential).T
        term = Angular(form, ql, 256)
        first, second = gather_table(angular_table[0].T)

        def angular(points, plus=None):
            acc = term.call(first[0], points, first[1], pot)
            return term.call(second[0], points, second[1], pot, acc=acc, plus=plus, scale=c)
    else:
        table = lax.all_gather(angular_table[0], "grid", axis=1, tiled=True)

        def angular(points, plus=None):
            x = form.unpack_rows(points)
            values = lax.dot_general(table, x, (((0,), (0,)), ((), ())), precision=high) * potential
            return form.pack_rows(jnp.dot(table, values, precision=high), c, plus)

    def neighbours(x):
        if K == 2:
            return lax.ppermute(x, "hel", [(0, 1), (1, 0)]), c * jnp.where(k == 0, coup_above, coup)[:, None]
        below = from_behind(x, "hel", 1)
        above = from_behind(x, "hel", -1)
        below, above = (form.unpack(v) if v.ndim > 2 else v for v in (below, above))
        return coup[:, None] * below + coup_above[:, None] * above, jnp.full((jl, 1), c, jnp.float32)

    def radial(x):
        grid3 = x.reshape(jl, RB, RS)
        out = jnp.einsum("ab,jbs->jas", kin_big, grid3, precision=high)
        out = out + jnp.einsum("st,jat->jas", kin_small, grid3, precision=high)
        return out.reshape(jl, nr)

    older, newer = prev, now
    packed = form.pack(newer)
    points = exchange(packed)
    got, factor = neighbours(newer)
    for _ in range(STEPS - 1):
        base = radial(newer)
        base = c * (base + diag * newer) - older
        w = form.pack_linked(base, got, factor, cent)
        w = exchange(w)
        points = angular(points)
        points = w + points
        packed = exchange(points)
        got, factor = neighbours(packed)
        older, newer = newer, form.unpack(packed)
    ret = angular(points)
    ret = exchange(ret)
    base = radial(newer)
    base = c * (base + diag * newer) - older
    older, newer = newer, form.unpack_linked(ret, base, got, factor, cent)
    return older[None], newer[None]


def solution(mesh):
    return jax.shard_map(
        shards,
        mesh=mesh,
        in_specs=(
            P("hel", "grid", None),
            P("hel", "grid", None),
            P("hel", None, "grid"),
            P(None, "grid"),
            P("hel", "grid"),
            P(),
            P("hel", "grid"),
            P(),
        ),
        out_specs=(P("hel", "grid", None), P("hel", "grid", None)),
        check_vma=False,
    )
```
